32 devices in a mesh: grp: 2 (over y), visit: 4 (over z), tile: 2 (over x), band: 2 (over core).
Axes of the slice: x: 2, y: 2, z: 4, core: 2. Of those that a mesh axis runs over, the one named last changes fastest.
Arguments:
- template: bfloat16 [256, 512], P(('grp', 'tile', 'band'), 'visit'), parts along dimension 0, may hold values from -6 to 6
- images: bfloat16 [8, 128, 512], P(('grp', 'visit'), ('tile', 'band')), parts along dimension 0, may hold values from -6 to 6
- basis_taps: float32 [3, 19], replicated
- psf_taps: float32 [2, 19], replicated
- coeffs: float32 [8, 3, 6], P('grp'), parts along dimension 0, may hold values from -3 to 3
- offsets: int32 [8, 2], P('grp'), parts along dimension 0, may hold values from -8 to 8, as said below
- intersection: int32 [8, 4], P('grp'), parts along dimension 0, may hold values from 0 to 1, as said below
- weights: float32 [8], P('grp'), parts along dimension 0, may hold values from 0.5 to 4
Outputs:
- coadd: float32 [256, 512], P(('grp', 'tile', 'band'), 'visit'), parts along dimension 0
The draws below stay inside these ranges and needn't reach their ends.
There are 2 independent parts, one for each index of `grp`. The reference program is written for one: setup_inputs(seed, part) draws one part's arguments, and reference() takes and returns one part's arrays. A program takes and returns all parts, laid end to end along the dimension named above; an argument that names none is the same for every part. Nothing has to cross between parts.
Inputs may be any that keep to these rules, and one draw needn't show every extreme that they name: `offsets`: some visit has row offset 8 and some visit has column offset -8. `intersection`: every slab is covered by at least one visit.
All inputs are finite; a program needn't handle non-finite values.
Results may differ from the reference program's by a relative error of at most 0.00069.
Values may be sent and summed in bfloat16 or wider, within the bound.
A program may use at most 64 MiB of HBM per device.

```python
import math
import jax
import jax.numpy as jnp
from jax import lax

SLAB_ROWS = 32
BASES = 3
TERMS = 6
TAPS = 19
SHIFT = 8
SLABS = 4
PATCH_ROWS = 128
PATCH_COLS = 512
VISITS = 4


def profile_rows(key_widths, rows_count, lower, upper):
    widths_drawn = jax.random.uniform(key_widths, (rows_count, 1), jnp.float32, lower, upper)
    positions = jnp.arange(TAPS, dtype=jnp.float32) - TAPS // 2
    return jnp.exp(-positions * positions / (2.0 * widths_drawn * widths_drawn)) / widths_drawn


def draw_basis_taps(key, part):
    key_widths = jax.random.fold_in(key, 11)
    return profile_rows(key_widths, BASES, 2.0, 6.0)


def draw_psf_taps(key, part):
    key_widths = jax.random.fold_in(key, 13)
    return profile_rows(key_widths, 2, 2.5, 5.0)


def draw_offsets(key, part):
    shifts = jax.random.randint(jax.random.fold_in(key, 21), (VISITS, 2), -SHIFT, SHIFT + 1)
    row_pick = jax.random.randint(jax.random.fold_in(key, 22), (), 0, VISITS)
    col_pick = jax.random.randint(jax.random.fold_in(key, 23), (), 0, VISITS)
    shifts = shifts.at[row_pick, 0].set(SHIFT)
    shifts = shifts.at[col_pick, 1].set(-SHIFT)
    return shifts.astype(jnp.int32)


def draw_intersection(key, part):
    levels = jax.random.randint(jax.random.fold_in(key, 31), (VISITS, 1), 1, 5)
    dice_rolls = jax.random.randint(jax.random.fold_in(key, 32), (VISITS, SLABS), 0, 4)
    covered = (dice_rolls < levels).astype(jnp.int32)
    owners = jax.random.randint(jax.random.fold_in(key, 33), (SLABS,), 0, VISITS)
    forced = (jnp.arange(VISITS, dtype=jnp.int32)[:, None] == owners[None, :]).astype(jnp.int32)
    return jnp.maximum(covered, forced)


def block_scale(own_key, extent, shards, least, largest):
    loudness, own = 1.0, jax.random.fold_in(own_key, 6)
    for dim, parts in shards:
        draws = jnp.exp(jax.random.uniform(jax.random.fold_in(own, dim), (parts,), jnp.float32, least / len(shards), largest / len(shards)))
        loudness = loudness * jnp.repeat(draws, extent[dim] // parts).reshape([-1 if axis == dim else 1 for axis in range(len(extent))])
    return loudness


def scatter_about(key, extent, spread, reach, split=(), held_as=jnp.bfloat16):
    result = jax.random.normal(key, extent, jnp.float32) * spread
    if len(split) > 0:
        result = block_scale(key, extent, split, -0.22, 0.18) * result
    return jnp.clip(result, min=-reach, max=reach).astype(held_as)


def setup_inputs(seed: int = 0, part: int = 0) -> dict:
    seeds = jax.random.split(jax.random.key(seed), 9)
    part_keys = jax.random.split(jax.random.fold_in(seeds[8], part), 9)
    template = scatter_about(part_keys[0], (PATCH_ROWS, PATCH_COLS), 1.0, 6.0, ((0, 4), (1, 4)))
    images = scatter_about(part_keys[1], (VISITS, PATCH_ROWS, PATCH_COLS), 1.0, 6.0, ((0, 4), (1, 4)))
    basis_taps = draw_basis_taps(jax.random.fold_in(seeds[8], 71), part)
    psf_taps = draw_psf_taps(jax.random.fold_in(seeds[8], 71), part)
    coeffs = scatter_about(part_keys[4], (VISITS, BASES, TERMS), 0.5, 3.0, (), jnp.float32)
    offsets = draw_offsets(jax.random.fold_in(jax.random.fold_in(seeds[8], part), 71), part)
    intersection = draw_intersection(jax.random.fold_in(jax.random.fold_in(seeds[8], part), 71), part)
    weights = jnp.clip(jnp.exp(jax.random.uniform(part_keys[7], (VISITS,), jnp.float32, math.log(0.5), math.log(4.0))), 0.5, 4.0)
    return dict(template=template, images=images, basis_taps=basis_taps, psf_taps=psf_taps, coeffs=coeffs, offsets=offsets, intersection=intersection, weights=weights)


def slide_valid(values, kernel, direction):
    length = values.shape[direction] - TAPS + 1
    summed = kernel[0] * lax.slice_in_dim(values, 0, length, axis=direction)
    for tap_index in range(1, TAPS):
        summed = summed + kernel[tap_index] * lax.slice_in_dim(values, tap_index, tap_index + length, axis=direction)
    return summed


def slide_same(values, kernel, direction):
    radius = TAPS // 2
    widths = [(0, 0)] * values.ndim
    widths[direction] = (radius, radius)
    return slide_valid(jnp.pad(values, widths), kernel, direction)


def reference(template, images, basis_taps, psf_taps, coeffs, offsets, intersection, weights):
    patch_rows, patch_cols = template.shape
    smooth_in = template.astype(jnp.float32)
    planes = []
    for basis_index in range(BASES):
        smoothed = slide_same(slide_same(smooth_in, basis_taps[basis_index], 0), basis_taps[basis_index], 1)
        planes.append(smoothed.astype(jnp.bfloat16))
    basis_planes = jnp.pad(jnp.stack(planes), ((0, 0), (SHIFT, SHIFT), (SHIFT, SHIFT)))
    row_coord = (jnp.arange(patch_rows).astype(jnp.float32) + 0.5) * (2.0 / patch_rows) - 1.0
    col_coord = (jnp.arange(patch_cols).astype(jnp.float32) + 0.5) * (2.0 / patch_cols) - 1.0
    row_grid = jnp.broadcast_to(row_coord[:, None], (patch_rows, patch_cols))
    col_grid = jnp.broadcast_to(col_coord[None, :], (patch_rows, patch_cols))
    poly_terms = jnp.stack([jnp.ones_like(col_grid), col_grid, row_grid, col_grid * col_grid, col_grid * row_grid, row_grid * row_grid])
    slab_of_row = jnp.arange(patch_rows) // SLAB_ROWS

    def visit_term(running, inputs):
        visit_image, visit_coeffs, visit_offset, visit_intersection, weight = inputs
        shifted = lax.dynamic_slice(basis_planes, (jnp.int32(0), SHIFT + visit_offset[0], SHIFT + visit_offset[1]), (BASES, patch_rows, patch_cols))
        shifted = lax.optimization_barrier(shifted).astype(jnp.float32)
        fields = jnp.einsum("bq,qyx->byx", visit_coeffs, poly_terms, precision=lax.Precision.HIGHEST)
        model_image = jnp.sum(fields * shifted, axis=0)
        difference = lax.optimization_barrier((visit_image.astype(jnp.float32) - model_image).astype(jnp.bfloat16)).astype(jnp.float32)
        filtered = slide_same(slide_same(difference, psf_taps[0], 0), psf_taps[1], 1)
        row_weight = weight * visit_intersection[slab_of_row].astype(jnp.float32)
        return running + filtered * row_weight[:, None], None

    numerator, _ = lax.scan(visit_term, jnp.zeros((patch_rows, patch_cols), jnp.float32), (images, coeffs, offsets, intersection, weights))
    denominator = jnp.sum(weights[:, None] * intersection.astype(jnp.float32), axis=0)[slab_of_row]
    return numerator / denominator[:, None]
```

```python
import functools

import jax
import jax.numpy as jnp
from jax import lax
from jax.experimental import pallas as pl
from jax.experimental.pallas import tpu as pltpu
from jax.sharding import PartitionSpec as P

BASES = 3
TAPS = 19
RADIUS = TAPS // 2
SHIFT = 8
LANES = 128
WIDE = 2 * LANES
HALO = 16
F32 = jnp.float32
BF16 = jnp.bfloat16


def split(x):
    high = x.astype(BF16)
    return high, (x - high.astype(F32)).astype(BF16)


def mm(a, b):
    return jnp.dot(a, b, preferred_element_type=F32)


def mm_split(a, b):
    a_high, a_low = split(a)
    b_high, b_low = split(b)
    return mm(a_high, b_high) + (mm(a_high, b_low) + mm(a_low, b_high))


def band(taps, row, rows, width, start, flip):
    lane = lax.broadcasted_iota(jnp.int32, (8, width), 1)
    line = jnp.zeros((8, width), F32)
    for t in range(TAPS):
        d = (RADIUS - t) if flip else (t - RADIUS)
        line = jnp.where(lane == d % width, taps[row, t], line)
    full = jnp.broadcast_to(line[:1], (rows, width))
    return pltpu.roll(full, start % width, 1, stride=1, stride_axis=0)


def pack(block, first):
    groups = block.shape[0] // 8
    width = LANES // groups
    lane = lax.broadcasted_iota(jnp.int32, (8, LANES), 1)
    packed = None
    for g in range(groups):
        part = pltpu.roll(block[8 * g:8 * g + 8], (width * g - first) % LANES, 1)
        packed = part if packed is None else jnp.where(lane < width * g, packed, part)
    return packed.astype(BF16)


def unpack(packed, first, groups, count):
    width = LANES // count
    packed = packed.astype(F32)
    return [pltpu.roll(packed, (first - width * g) % LANES, 1) for g in groups]


def kernel(
    sizes,
    template, images, *small,
):
    small, (
        out,
        image, basis_taps, psf_taps, coeffs, offsets, cover, weights,
        tiles, windows, packs, tile_packs, tile_sides, cols_high, cols_low,
        loaded, sent_tiles, got_tiles, sent_windows, got_windows, ready,
    ) = small[:6], small[6:]
    visits, slabs, bands = sizes
    slab_rows = template.shape[0]
    groups, halo = slab_rows // 8, HALO // 8
    main = 1 + halo
    below_main = main + groups + 1
    patch_rows, patch_cols = slab_rows * slabs, images.shape[3]
    me = lax.axis_index("visit")
    slab = lax.axis_index("tile") * bands + lax.axis_index("band")

    def place(visit, row):
        return {"visit": visit, "tile": lax.div(row, bands), "band": lax.rem(row, bands)}

    above, below = slab > 0, slab < slabs - 1

    loads = [
        pltpu.make_async_copy(source, target, loaded.at[i])
        for i, (source, target) in enumerate(
            zip(
                (images.at[0], template, *small),
                (image, tiles.at[1], basis_taps, psf_taps, coeffs, offsets, cover, weights),
            )
        )
    ]
    for load in loads[:2]:
        load.start()

    beside = above.astype(jnp.int32) + below.astype(jnp.int32)

    def greet(semaphore, other, beyond, row):
        pl.semaphore_signal(semaphore, 1, device_id=place(other, slab))
        pl.when(beyond)(lambda: pl.semaphore_signal(semaphore, 1, device_id=place(other, row)))

    barrier = pltpu.get_barrier_semaphore()
    pl.when(below)(lambda: pl.semaphore_signal(barrier, 1, device_id=place(me, slab + 1)))
    for b in range(visits):
        pl.when(me < b)(lambda b=b: greet(barrier, jnp.int32(b), below, slab + 1))

    for load in loads[2:]:
        load.start()

    for dr in (-1, 0, 1):
        for dc in (-1, 0, 1):
            if (dr, dc) == (0, 0):
                continue
            missing = jnp.logical_or(
                jnp.logical_or(slab + dr < 0, slab + dr >= slabs),
                jnp.logical_or(me + dc < 0, me + dc >= visits),
            )

            def blank(dr=dr, dc=dc):
                if dc == 0:
                    tiles[1 + dr] = jnp.zeros((slab_rows, LANES), BF16)
                else:
                    tile_sides[(1 + dc) // 2, 1 + dr] = jnp.zeros((8, LANES), BF16)

            pl.when(missing)(blank)

    ahead = me * (1 + above.astype(jnp.int32)) + above.astype(jnp.int32)
    pl.when(ahead > 0)(lambda: pl.semaphore_wait(barrier, ahead))
    pl.when(above)(lambda: pl.semaphore_signal(ready.at[me], 1, device_id=place(me, slab - 1)))
    for b in range(visits):
        pl.when(me > b)(lambda b=b: greet(ready.at[me], jnp.int32(b), above, slab - 1))

    loads[1].wait()
    own = tiles[1].astype(F32)
    tile_packs[0] = pack(own, 0)
    tile_packs[1] = pack(own, LANES - LANES // groups)
    loads[0].wait()
    lane = lax.broadcasted_iota(jnp.int32, (slab_rows, LANES), 1)
    blocks = [image[:, :, b * LANES:(b + 1) * LANES].astype(F32).reshape(slab_rows, LANES) for b in range(visits)]
    for b in range(visits):
        right, left = blocks[min(b + 1, visits - 1)], blocks[max(b - 1, 0)]
        packs[b] = pack(jnp.where(lane < LANES // 2, right, left), -LANES // groups // 2)

    def tile_copy(dr, dc):
        if dc == 0:
            source, target = tiles.at[1], tiles.at[1 - dr]
        else:
            source, target = tile_packs.at[(1 + dc) // 2], tile_sides.at[(1 - dc) // 2, 1 - dr]
        return pltpu.make_async_remote_copy(
            src_ref=source,
            dst_ref=target,
            send_sem=sent_tiles.at[1 + dc],
            recv_sem=got_tiles.at[1 - dc],
            device_id=place(me + dc, slab + dr),
        )

    def window_copy(other, dr):
        if dr == 0:
            first, height, target = 0, groups, main
        elif dr < 0:
            first, height, target = 0, halo, below_main
        else:
            first, height, target = groups - halo, halo, 1
        return pltpu.make_async_remote_copy(
            src_ref=image.at[pl.ds(first, height), :, pl.ds(pl.multiple_of(other * LANES, LANES), LANES)],
            dst_ref=windows.at[me, pl.ds(target, height)],
            send_sem=sent_windows.at[other],
            recv_sem=got_windows.at[me],
            device_id=place(other, slab + dr),
        )

    def side_copy(other, dr):
        return pltpu.make_async_remote_copy(
            src_ref=packs.at[other],
            dst_ref=windows.at[me, (below_main + halo, main + groups, 0)[1 + dr]],
            send_sem=sent_windows.at[other],
            recv_sem=got_windows.at[me],
            device_id=place(other, slab + dr),
        )

    def nearest(k):
        both = 2 * jnp.minimum(me, visits - 1 - me)
        paired = me + ((k + 1) // 2) * (1 if k % 2 == 0 else -1)
        rest = jnp.where(2 * me < visits - 1, k, visits - 1 - k)
        return jnp.where(k <= both, paired, rest)


    def await_bytes(ref, size, sem):
        if size > 0:
            part = ref.at[pl.ds(0, size)]
            pltpu.make_async_copy(part, part, sem).wait()

    def await_windows(sems, other):
        for near in range(3):
            for own in (False, True):
                size = near * (halo + 1) + (0 if own else groups + 1)
                pl.when(jnp.logical_and(beside == near, (other == me) == own))(
                    lambda size=size: await_bytes(windows.at[other], size, sems.at[other])
                )

    def await_tiles(sems):
        for dc in (0, -1, 1):
            there = jnp.logical_and(me + dc >= 0, me + dc < visits)
            for near in range(3):
                ref, size = (tiles, near) if dc == 0 else (tile_sides.at[0], near + 1)
                pl.when(jnp.logical_and(beside == near, there))(
                    lambda ref=ref, size=size, dc=dc: await_bytes(ref, size, sems.at[1 + dc])
                )

    def send_window(other, dr):
        side_copy(other, dr).start()
        window_copy(other, dr).start()

    def send_windows(other, rows=(0, -1, 1)):
        for dr in rows:
            if dr == 0:
                send_window(other, 0)
            else:
                pl.when(above if dr < 0 else below)(lambda dr=dr: send_window(other, dr))

    def send_tiles(dc, rows=(0, -1, 1)):
        for dr in rows:
            if dr == 0:
                tile_copy(0, dc).start()
            else:
                pl.when(above if dr < 0 else below)(lambda dr=dr: tile_copy(dr, dc).start())

    def send_row(dr):
        tile_copy(dr, 0).start()
        send_window(me, dr)

    def await_ready(other):
        pl.semaphore_wait(ready.at[other], 1 + below.astype(jnp.int32))

    def send_ahead(rows):
        for b in range(visits - 2):
            pl.when(me > b + 1)(lambda b=b: send_windows(jnp.int32(b), rows))
        pl.when(me > 0)(lambda: send_tiles(-1, rows))
        pl.when(me > 0)(lambda: send_windows(me - 1, rows))

    pl.when(above)(lambda: send_row(-1))
    send_ahead((-1, 0))

    windows[me, main:main + groups] = image[:, :, pl.ds(pl.multiple_of(me * LANES, LANES), LANES)]
    windows[me, main + groups] = packs[me]
    for load in loads[2:]:
        load.wait()

    out_rows = slab_rows + 2 * (HALO + SHIFT)
    in_rows = 3 * slab_rows
    first = slab_rows - HALO - SHIFT
    rows_parts = []
    for b in range(BASES):
        rows_parts.append(split(band(basis_taps, b, out_rows, LANES, first, False)[:, :in_rows]))
        high, low = split(band(basis_taps, b, WIDE, WIDE, 0, True))
        cols_high[b], cols_low[b] = high, low
    psf_rows = band(psf_taps, 0, slab_rows, LANES, HALO, False)[:, :slab_rows + 2 * HALO]
    high, low = split(band(psf_taps, 1, WIDE, WIDE, 0, True)[:, :LANES])
    cols_high[BASES, :, :LANES], cols_low[BASES, :, :LANES] = high, low

    column = lax.broadcasted_iota(jnp.int32, (8, WIDE), 1)
    column = jnp.where(column < WIDE - LANES // 2, column, column - WIDE) + me * LANES
    inside_cols = jnp.logical_and(column >= 0, column < patch_cols)[:1]
    column = column.astype(F32)[:1]
    row = lax.broadcasted_iota(jnp.int32, (out_rows, LANES), 0) + (slab * slab_rows - HALO - SHIFT)
    inside_rows = jnp.logical_and(row >= 0, row < patch_rows)
    row = row.astype(F32)

    def send_below():
        pl.semaphore_wait(ready.at[me], 1)
        send_row(1)
        send_ahead((1,))

    pl.when(below)(send_below)

    def send_next():
        await_ready(me + 1)
        send_tiles(1)
        send_windows(me + 1)

    pl.when(me < visits - 1)(send_next)

    def send_far(other):
        await_ready(other)
        send_windows(other)

    pl.when(me + 2 < visits)(lambda: send_far(me + 2))

    for b in range(3, visits):
        pl.when(me + 2 < b)(lambda b=b: send_far(jnp.int32(b)))

    await_tiles(got_tiles)
    lane = lax.broadcasted_iota(jnp.int32, (in_rows, LANES), 1)
    every, width = range(groups), LANES // groups
    centre = tiles[...].astype(F32).reshape(in_rows, LANES)
    right, left = [], []
    for part in range(3):
        left += unpack(tile_sides[0, part], LANES - width, every, groups)
        right += unpack(tile_sides[1, part], 0, every, groups)
    right, left = jnp.concatenate(right, axis=0), jnp.concatenate(left, axis=0)
    field = jnp.concatenate([centre, jnp.where(lane < LANES // 2, right, left)], axis=1).astype(BF16)
    planes = []
    inside = jnp.logical_and(jnp.concatenate([inside_rows, inside_rows], axis=1), inside_cols)
    for b in range(BASES):
        high, low = rows_parts[b]
        passed = mm(high, field) + mm(low, field)
        high, low = split(passed)
        plane = mm(high, cols_high[b]) + (mm(high, cols_low[b]) + mm(low, cols_high[b]))
        planes.append(jnp.where(inside, plane, 0.0).astype(BF16).astype(F32))

    window_rows = slab_rows + 2 * HALO
    denominator = jnp.float32(0)
    total = jnp.zeros((window_rows, WIDE), F32)
    models = []
    for k in range(visits):
        source = nearest(k)
        dy, dx = offsets[0, source], offsets[1, source]
        u = (column - dx.astype(F32) + 0.5) * (2.0 / patch_cols) - 1.0
        w = (row - dy.astype(F32) + 0.5) * (2.0 / patch_rows) - 1.0
        model = None
        for b in range(BASES):
            c = [coeffs[b, source, q] for q in range(6)]
            still = c[0] + w * (c[2] + c[5] * w)
            slope = c[1] + c[4] * w
            both = lambda x: jnp.concatenate([x, x], axis=1)
            term = (both(still) + u * (both(slope) + c[3] * u)) * planes[b]
            model = term if model is None else model + term
        moved = pltpu.roll(model, out_rows - SHIFT - dy, 0)[:window_rows]
        models.append(pltpu.roll(moved, jnp.where(dx > 0, WIDE - dx, -dx), 1))

    for k in range(visits):
        source = nearest(k)
        await_windows(got_windows, source)
        window = windows[source].astype(F32)
        columns = []
        for part, chosen in (
            (0, every[-halo:]), (main + groups, every), (below_main + halo, every[:halo])
        ):
            columns += unpack(windows[source, part], -(width // 2), chosen, groups)
        blocks = [window[1:main + groups], window[below_main:below_main + halo]]
        seen = jnp.concatenate(
            [
                jnp.concatenate(blocks, axis=0).reshape(window_rows, LANES),
                jnp.concatenate(columns, axis=0),
            ],
            axis=1,
        )
        difference = (seen - models[k]).astype(BF16).astype(F32)
        weight = weights[source] * cover[source, slab].astype(F32)
        denominator = denominator + weight
        total = total + weight * difference

    y = lax.broadcasted_iota(jnp.int32, (window_rows, WIDE), 0) + (slab * slab_rows - HALO)
    total = jnp.where(
        jnp.logical_and(jnp.logical_and(y >= 0, y < patch_rows), inside_cols), total, 0.0
    )
    passed = mm_split(psf_rows, total)
    high, low = split(passed)
    psf_high, psf_low = cols_high[BASES, :, :LANES], cols_low[BASES, :, :LANES]
    filtered = mm(high, psf_high) + (mm(high, psf_low) + mm(low, psf_high))
    out[...] = filtered / jnp.full(filtered.shape, denominator, F32)
    await_tiles(sent_tiles)
    for b in range(visits):
        await_windows(sent_windows, jnp.int32(b))


def solution(mesh):
    visits, bands = mesh.shape["visit"], mesh.shape["band"]
    slabs = mesh.shape["tile"] * bands

    def shards(template, images, basis_taps, psf_taps, coeffs, offsets, cover, weights):
        slab_rows = template.shape[0]
        images = images.reshape(images.shape[0], slab_rows // 8, 8, images.shape[2])
        vmem = pl.BlockSpec(memory_space=pltpu.VMEM)
        small = (
            basis_taps, psf_taps, coeffs.transpose(1, 0, 2), offsets.transpose(1, 0), cover, weights
        )
        return pl.pallas_call(
            functools.partial(kernel, (visits, slabs, bands)),
            out_shape=pltpu.VMEM(template.shape, F32),
            in_specs=[pl.BlockSpec(memory_space=pl.ANY)] * 8,
            out_specs=vmem,
            scratch_shapes=[
                pltpu.VMEM(images.shape[1:], BF16),
                *[pltpu.SMEM(x.shape, x.dtype) for x in small],
                pltpu.VMEM((3, slab_rows, LANES), BF16),
                pltpu.VMEM((visits, (slab_rows + 2 * HALO) // 8 + 3, 8, LANES), BF16),
                pltpu.VMEM((visits, 8, LANES), BF16),
                pltpu.VMEM((2, 8, LANES), BF16),
                pltpu.VMEM((2, 3, 8, LANES), BF16),
                pltpu.VMEM((BASES + 1, WIDE, WIDE), BF16),
                pltpu.VMEM((BASES + 1, WIDE, WIDE), BF16),
                pltpu.SemaphoreType.DMA((8,)),
                pltpu.SemaphoreType.DMA((3,)),
                pltpu.SemaphoreType.DMA((3,)),
                pltpu.SemaphoreType.DMA((visits,)),
                pltpu.SemaphoreType.DMA((visits,)),
                pltpu.SemaphoreType.REGULAR((visits,)),
            ],
            compiler_params=pltpu.CompilerParams(collective_id=0, has_side_effects=True),
            name="coadd",
        )(template, images, *small)

    placed = (
        P(("grp", "tile", "band"), "visit"),
        P(("grp", "visit"), ("tile", "band"), None),
        P(),
        P(),
        P("grp", None, None),
        P("grp", None),
        P("grp", None),
        P("grp"),
    )
    return jax.shard_map(
        shards,
        mesh=mesh,
        in_specs=placed,
        out_specs=P(("grp", "tile", "band"), "visit"),
        check_vma=False,
    )
```

```python
import functools

import jax
import jax.numpy as jnp
from jax import lax
from jax.experimental import pallas as pl
from jax.experimental.pallas import tpu as pltpu
from jax.sharding import PartitionSpec as P

BASES = 3
TAPS = 19
RADIUS = TAPS // 2
SHIFT = 8
LANES = 128
WIDE = 2 * LANES
HALO = 16
F32 = jnp.float32
BF16 = jnp.bfloat16


def split(x):
    high = x.astype(BF16)
    return high, (x - high.astype(F32)).astype(BF16)


def mm(a, b):
    return jnp.dot(a, b, preferred_element_type=F32)


def mm_split(a, b):
    a_high, a_low = split(a)
    b_high, b_low = split(b)
    return mm(a_high, b_high) + (mm(a_high, b_low) + mm(a_low, b_high))


def band(taps, row, rows, width, start, flip):
    lane = lax.broadcasted_iota(jnp.int32, (8, width), 1)
    line = jnp.zeros((8, width), F32)
    for t in range(TAPS):
        d = (RADIUS - t) if flip else (t - RADIUS)
        line = jnp.where(lane == d % width, taps[row, t], line)
    full = jnp.broadcast_to(line[:1], (rows, width))
    return pltpu.roll(full, start % width, 1, stride=1, stride_axis=0)


def pack(block, first):
    groups = block.shape[0] // 8
    width = LANES // groups
    lane = lax.broadcasted_iota(jnp.int32, (8, LANES), 1)
    packed = None
    for g in range(groups):
        part = pltpu.roll(block[8 * g:8 * g + 8], (width * g - first) % LANES, 1)
        packed = part if packed is None else jnp.where(lane < width * g, packed, part)
    return packed.astype(BF16)


def unpack(packed, first, groups, count):
    width = LANES // count
    packed = packed.astype(F32)
    return [pltpu.roll(packed, (first - width * g) % LANES, 1) for g in groups]


def kernel(
    sizes,
    template, images, *small,
):
    small, (
        out,
        image, basis_taps, psf_taps, coeffs, offsets, cover, weights,
        tiles, windows, packs, tile_packs, tile_sides, cols_high, cols_low,
        loaded, counted, sent, got_tiles, got_windows, ready,
    ) = small[:6], small[6:]
    visits, slabs, bands = sizes
    slab_rows = template.shape[0]
    groups, halo = slab_rows // 8, HALO // 8
    main = 1 + halo
    below_main = main + groups + 1
    patch_rows, patch_cols = slab_rows * slabs, images.shape[3]
    me = lax.axis_index("visit")
    slab = lax.axis_index("tile") * bands + lax.axis_index("band")

    def place(visit, row):
        return {"visit": visit, "tile": lax.div(row, bands), "band": lax.rem(row, bands)}

    above, below = slab > 0, slab < slabs - 1

    loads = [
        pltpu.make_async_copy(source, target, loaded.at[min(i // 2, 1)])
        for i, (source, target) in enumerate(
            zip(
                (images.at[0], template, *small),
                (image, tiles.at[1], basis_taps, psf_taps, coeffs, offsets, cover, weights),
            )
        )
    ]
    for load in loads[:2]:
        load.start()

    beside = above.astype(jnp.int32) + below.astype(jnp.int32)

    def greet(semaphore, other, beyond, row):
        pl.semaphore_signal(semaphore, 1, device_id=place(other, slab))
        pl.when(beyond)(lambda: pl.semaphore_signal(semaphore, 1, device_id=place(other, row)))

    barrier = pltpu.get_barrier_semaphore()
    pl.when(below)(lambda: pl.semaphore_signal(barrier, 1, device_id=place(me, slab + 1)))
    for b in range(visits):
        pl.when(me < b)(lambda b=b: greet(barrier, jnp.int32(b), below, slab + 1))

    for load in loads[2:]:
        load.start()

    for dr in (-1, 0, 1):
        for dc in (-1, 0, 1):
            if (dr, dc) == (0, 0):
                continue
            missing = jnp.logical_or(
                jnp.logical_or(slab + dr < 0, slab + dr >= slabs),
                jnp.logical_or(me + dc < 0, me + dc >= visits),
            )

            def blank(dr=dr, dc=dc):
                if dc == 0:
                    tiles[1 + dr] = jnp.zeros((slab_rows, LANES), BF16)
                else:
                    tile_sides[(1 + dc) // 2, 1 + dr] = jnp.zeros((8, LANES), BF16)

            pl.when(missing)(blank)

    ahead = me * (1 + above.astype(jnp.int32)) + above.astype(jnp.int32)
    pl.when(ahead > 0)(lambda: pl.semaphore_wait(barrier, ahead))
    pl.when(above)(lambda: pl.semaphore_signal(ready.at[me], 1, device_id=place(me, slab - 1)))
    for b in range(visits):
        pl.when(me > b)(lambda b=b: greet(ready.at[me], jnp.int32(b), above, slab - 1))

    def await_bytes(ref, size, sem):
        if size > 0:
            part = ref.at[pl.ds(0, size)]
            pltpu.make_async_copy(part, part, sem).wait()

    await_bytes(counted, groups * (1 + visits), loaded.at[0])

    def tile_copy(dr, dc):
        if dc == 0:
            source, target = tiles.at[1], tiles.at[1 - dr]
        else:
            source, target = tile_packs.at[(1 + dc) // 2], tile_sides.at[(1 - dc) // 2, 1 - dr]
        return pltpu.make_async_remote_copy(
            src_ref=source,
            dst_ref=target,
            send_sem=sent.at[0],
            recv_sem=got_tiles.at[0],
            device_id=place(me + dc, slab + dr),
        )

    def window_copy(other, dr):
        if dr == 0:
            first, height, target = 0, groups, main
        elif dr < 0:
            first, height, target = 0, halo, below_main
        else:
            first, height, target = groups - halo, halo, 1
        return pltpu.make_async_remote_copy(
            src_ref=image.at[pl.ds(first, height), :, pl.ds(pl.multiple_of(other * LANES, LANES), LANES)],
            dst_ref=windows.at[me, pl.ds(target, height)],
            send_sem=sent.at[0],
            recv_sem=got_windows.at[me],
            device_id=place(other, slab + dr),
        )

    def side_copy(other, dr):
        return pltpu.make_async_remote_copy(
            src_ref=packs.at[other],
            dst_ref=windows.at[me, (below_main + halo, main + groups, 0)[1 + dr]],
            send_sem=sent.at[0],
            recv_sem=got_windows.at[me],
            device_id=place(other, slab + dr),
        )

    def nearest(k):
        both = 2 * jnp.minimum(me, visits - 1 - me)
        paired = me + ((k + 1) // 2) * (1 if k % 2 == 0 else -1)
        rest = jnp.where(2 * me < visits - 1, k, visits - 1 - k)
        return jnp.where(k <= both, paired, rest)


    def await_windows(sems, other):
        for near in range(3):
            for own in (False, True):
                size = near * (halo + 1) + (0 if own else groups + 1)
                pl.when(jnp.logical_and(beside == near, (other == me) == own))(
                    lambda size=size: await_bytes(windows.at[other], size, sems.at[other])
                )

    def await_blocks(sem, blocks):
        sides = (me > 0).astype(jnp.int32) + (me < visits - 1).astype(jnp.int32)
        for near in range(3):
            for wide in range(3):
                pl.when(jnp.logical_and(beside == near, sides == wide))(
                    lambda size=blocks(near, wide): await_bytes(counted, size, sem)
                )

    def tile_blocks(near, wide):
        return near * groups + wide * (1 + near)

    def sent_blocks(near, wide):
        return tile_blocks(near, wide) + (visits - 1) * (groups + 1) + visits * near * (halo + 1)

    def send_window(other, dr):
        side_copy(other, dr).start()
        window_copy(other, dr).start()

    def send_windows(other, rows=(0, -1, 1)):
        for dr in rows:
            if dr == 0:
                send_window(other, 0)
            else:
                pl.when(above if dr < 0 else below)(lambda dr=dr: send_window(other, dr))

    def send_tiles(dc, rows=(0, -1, 1)):
        for dr in rows:
            if dr == 0:
                tile_copy(0, dc).start()
            else:
                pl.when(above if dr < 0 else below)(lambda dr=dr: tile_copy(dr, dc).start())

    def send_row(dr):
        tile_copy(dr, 0).start()
        send_window(me, dr)

    def await_ready(other):
        pl.semaphore_wait(ready.at[other], 1 + below.astype(jnp.int32))

    def send_next_ahead(rows):
        pl.when(me > 0)(lambda: send_tiles(-1, rows))
        pl.when(me > 0)(lambda: send_windows(me - 1, rows))

    def send_ahead(rows):
        for b in range(visits - 2):
            pl.when(me > b + 1)(lambda b=b: send_windows(jnp.int32(b), rows))
        send_next_ahead(rows)

    lane = lax.broadcasted_iota(jnp.int32, (slab_rows, LANES), 1)
    blocks = [image[:, :, b * LANES:(b + 1) * LANES].astype(F32).reshape(slab_rows, LANES) for b in range(visits)]
    for b in range(visits):
        right, left = blocks[min(b + 1, visits - 1)], blocks[max(b - 1, 0)]
        packs[b] = pack(jnp.where(lane < LANES // 2, right, left), -LANES // groups // 2)
        pl.when(me > b + 1)(lambda b=b: send_windows(jnp.int32(b), (-1, 0)))
    own = tiles[1].astype(F32)
    tile_packs[0] = pack(own, 0)
    tile_packs[1] = pack(own, LANES - LANES // groups)
    pl.when(above)(lambda: send_row(-1))
    send_next_ahead((-1, 0))

    windows[me, main:main + groups] = image[:, :, pl.ds(pl.multiple_of(me * LANES, LANES), LANES)]
    windows[me, main + groups] = packs[me]
    for load in loads[2:]:
        load.wait()

    out_rows = slab_rows + 2 * (HALO + SHIFT)
    in_rows = 3 * slab_rows
    first = slab_rows - HALO - SHIFT
    rows_parts = []
    for b in range(BASES):
        rows_parts.append(split(band(basis_taps, b, out_rows, LANES, first, False)[:, :in_rows]))
        high, low = split(band(basis_taps, b, WIDE, WIDE, 0, True))
        cols_high[b], cols_low[b] = high, low
    psf_rows = band(psf_taps, 0, slab_rows, LANES, HALO, False)[:, :slab_rows + 2 * HALO]
    high, low = split(band(psf_taps, 1, WIDE, WIDE, 0, True)[:, :LANES])
    cols_high[BASES, :, :LANES], cols_low[BASES, :, :LANES] = high, low

    column = lax.broadcasted_iota(jnp.int32, (8, WIDE), 1)
    column = jnp.where(column < WIDE - LANES // 2, column, column - WIDE) + me * LANES
    inside_cols = jnp.logical_and(column >= 0, column < patch_cols)[:1]
    column = column.astype(F32)[:1]
    row = lax.broadcasted_iota(jnp.int32, (out_rows, LANES), 0) + (slab * slab_rows - HALO - SHIFT)
    inside_rows = jnp.logical_and(row >= 0, row < patch_rows)
    row = row.astype(F32)

    def send_below():
        pl.semaphore_wait(ready.at[me], 1)
        send_row(1)
        send_ahead((1,))

    pl.when(below)(send_below)

    def send_next():
        await_ready(me + 1)
        send_tiles(1)
        send_windows(me + 1)

    pl.when(me < visits - 1)(send_next)

    def send_far(other):
        await_ready(other)
        send_windows(other)

    pl.when(me + 2 < visits)(lambda: send_far(me + 2))

    for b in range(3, visits):
        pl.when(me + 2 < b)(lambda b=b: send_far(jnp.int32(b)))

    await_blocks(got_tiles.at[0], tile_blocks)
    lane = lax.broadcasted_iota(jnp.int32, (in_rows, LANES), 1)
    every, width = range(groups), LANES // groups
    centre = tiles[...].astype(F32).reshape(in_rows, LANES)
    right, left = [], []
    for part in range(3):
        left += unpack(tile_sides[0, part], LANES - width, every, groups)
        right += unpack(tile_sides[1, part], 0, every, groups)
    right, left = jnp.concatenate(right, axis=0), jnp.concatenate(left, axis=0)
    field = jnp.concatenate([centre, jnp.where(lane < LANES // 2, right, left)], axis=1).astype(BF16)
    planes = []
    inside = jnp.logical_and(jnp.concatenate([inside_rows, inside_rows], axis=1), inside_cols)
    for b in range(BASES):
        high, low = rows_parts[b]
        passed = mm(high, field) + mm(low, field)
        high, low = split(passed)
        plane = mm(high, cols_high[b]) + (mm(high, cols_low[b]) + mm(low, cols_high[b]))
        planes.append(jnp.where(inside, plane, 0.0).astype(BF16).astype(F32))

    window_rows = slab_rows + 2 * HALO
    denominator = jnp.float32(0)
    total = jnp.zeros((window_rows, WIDE), F32)
    models = []
    for k in range(visits):
        source = nearest(k)
        dy, dx = offsets[0, source], offsets[1, source]
        u = (column - dx.astype(F32) + 0.5) * (2.0 / patch_cols) - 1.0
        w = (row - dy.astype(F32) + 0.5) * (2.0 / patch_rows) - 1.0
        model = None
        for b in range(BASES):
            c = [coeffs[b, source, q] for q in range(6)]
            still = c[0] + w * (c[2] + c[5] * w)
            slope = c[1] + c[4] * w
            both = lambda x: jnp.concatenate([x, x], axis=1)
            term = (both(still) + u * (both(slope) + c[3] * u)) * planes[b]
            model = term if model is None else model + term
        moved = pltpu.roll(model, out_rows - SHIFT - dy, 0)[:window_rows]
        models.append(pltpu.roll(moved, jnp.where(dx > 0, WIDE - dx, -dx), 1))

    for k in range(visits):
        source = nearest(k)
        await_windows(got_windows, source)
        window = windows[source].astype(F32)
        columns = []
        for part, chosen in (
            (0, every[-halo:]), (main + groups, every), (below_main + halo, every[:halo])
        ):
            columns += unpack(windows[source, part], -(width // 2), chosen, groups)
        blocks = [window[1:main + groups], window[below_main:below_main + halo]]
        seen = jnp.concatenate(
            [
                jnp.concatenate(blocks, axis=0).reshape(window_rows, LANES),
                jnp.concatenate(columns, axis=0),
            ],
            axis=1,
        )
        difference = (seen - models[k]).astype(BF16).astype(F32)
        weight = weights[source] * cover[source, slab].astype(F32)
        denominator = denominator + weight
        total = total + weight * difference

    y = lax.broadcasted_iota(jnp.int32, (window_rows, WIDE), 0) + (slab * slab_rows - HALO)
    total = jnp.where(
        jnp.logical_and(jnp.logical_and(y >= 0, y < patch_rows), inside_cols), total, 0.0
    )
    passed = mm_split(psf_rows, total)
    high, low = split(passed)
    psf_high, psf_low = cols_high[BASES, :, :LANES], cols_low[BASES, :, :LANES]
    filtered = mm(high, psf_high) + (mm(high, psf_low) + mm(low, psf_high))
    out[...] = filtered / jnp.full(filtered.shape, denominator, F32)
    await_blocks(sent.at[0], sent_blocks)


def solution(mesh):
    visits, bands = mesh.shape["visit"], mesh.shape["band"]
    slabs = mesh.shape["tile"] * bands

    def shards(template, images, basis_taps, psf_taps, coeffs, offsets, cover, weights):
        slab_rows = template.shape[0]
        images = images.reshape(images.shape[0], slab_rows // 8, 8, images.shape[2])
        groups, halo = slab_rows // 8, HALO // 8
        sent = 2 * groups + 6 + (visits - 1) * (groups + 1) + 2 * visits * (halo + 1)
        sent = max(sent, groups * (1 + images.shape[3] // LANES))
        vmem = pl.BlockSpec(memory_space=pltpu.VMEM)
        small = (
            basis_taps, psf_taps, coeffs.transpose(1, 0, 2), offsets.transpose(1, 0), cover, weights
        )
        return pl.pallas_call(
            functools.partial(kernel, (visits, slabs, bands)),
            out_shape=pltpu.VMEM(template.shape, F32),
            in_specs=[pl.BlockSpec(memory_space=pl.ANY)] * 8,
            out_specs=vmem,
            scratch_shapes=[
                pltpu.VMEM(images.shape[1:], BF16),
                *[pltpu.SMEM(x.shape, x.dtype) for x in small],
                pltpu.VMEM((3, slab_rows, LANES), BF16),
                pltpu.VMEM((visits, (slab_rows + 2 * HALO) // 8 + 3, 8, LANES), BF16),
                pltpu.VMEM((visits, 8, LANES), BF16),
                pltpu.VMEM((2, 8, LANES), BF16),
                pltpu.VMEM((2, 3, 8, LANES), BF16),
                pltpu.VMEM((BASES + 1, WIDE, WIDE), BF16),
                pltpu.VMEM((BASES + 1, WIDE, WIDE), BF16),
                pltpu.SemaphoreType.DMA((2,)),
                pltpu.VMEM((sent, 8, LANES), BF16),
                pltpu.SemaphoreType.DMA((1,)),
                pltpu.SemaphoreType.DMA((1,)),
                pltpu.SemaphoreType.DMA((visits,)),
                pltpu.SemaphoreType.REGULAR((visits,)),
            ],
            compiler_params=pltpu.CompilerParams(collective_id=0, has_side_effects=True),
            name="coadd",
        )(template, images, *small)

    placed = (
        P(("grp", "tile", "band"), "visit"),
        P(("grp", "visit"), ("tile", "band"), None),
        P(),
        P(),
        P("grp", None, None),
        P("grp", None),
        P("grp", None),
        P("grp"),
    )
    return jax.shard_map(
        shards,
        mesh=mesh,
        in_specs=placed,
        out_specs=P(("grp", "tile", "band"), "visit"),
        check_vma=False,
    )
```

```python
import functools

import jax
import jax.numpy as jnp
from jax import lax
from jax.experimental import pallas as pl
from jax.experimental.pallas import tpu as pltpu
from jax.sharding import PartitionSpec as P

BASES = 3
TAPS = 19
RADIUS = TAPS // 2
SHIFT = 8
LANES = 128
WIDE = 2 * LANES
HALO = 16
F32 = jnp.float32
BF16 = jnp.bfloat16


def split(x):
    high = x.astype(BF16)
    return high, (x - high.astype(F32)).astype(BF16)


def mm(a, b):
    return jnp.dot(a, b, preferred_element_type=F32)


def mm_split(a, b):
    a_high, a_low = split(a)
    b_high, b_low = split(b)
    return mm(a_high, b_high) + (mm(a_high, b_low) + mm(a_low, b_high))


def band(taps, row, rows, width, start, flip):
    lane = lax.broadcasted_iota(jnp.int32, (8, width), 1)
    line = jnp.zeros((8, width), F32)
    for t in range(TAPS):
        d = (RADIUS - t) if flip else (t - RADIUS)
        line = jnp.where(lane == d % width, taps[row, t], line)
    full = jnp.broadcast_to(line[:1], (rows, width))
    return pltpu.roll(full, start % width, 1, stride=1, stride_axis=0)


def pack(block, first):
    groups = block.shape[0] // 8
    width = LANES // groups
    lane = lax.broadcasted_iota(jnp.int32, (8, LANES), 1)
    packed = None
    for g in range(groups):
        part = pltpu.roll(block[8 * g:8 * g + 8], (width * g - first) % LANES, 1)
        packed = part if packed is None else jnp.where(lane < width * g, packed, part)
    return packed.astype(BF16)


def unpack(packed, first, groups, count):
    width = LANES // count
    packed = packed.astype(F32)
    return [pltpu.roll(packed, (first - width * g) % LANES, 1) for g in groups]


def kernel(
    sizes,
    template, images, *small,
):
    small, (
        out,
        image, basis_taps, psf_taps, coeffs, offsets, cover, weights,
        tiles, windows, packs, tile_packs, tile_sides, cols_high, cols_low,
        loaded, counted, got_tiles, got_windows, ready,
    ) = small[:6], small[6:]
    visits, slabs, bands = sizes
    slab_rows = template.shape[0]
    groups, halo = slab_rows // 8, HALO // 8
    main = 1 + halo
    below_main = main + groups + 1
    patch_rows, patch_cols = slab_rows * slabs, images.shape[3]
    me = lax.axis_index("visit")
    slab = lax.axis_index("tile") * bands + lax.axis_index("band")

    def place(visit, row):
        return {"visit": visit, "tile": lax.div(row, bands), "band": lax.rem(row, bands)}

    above, below = slab > 0, slab < slabs - 1

    loads = [
        pltpu.make_async_copy(source, target, loaded.at[min(i // 2, 1)])
        for i, (source, target) in enumerate(
            zip(
                (images.at[0], template, *small),
                (image, tiles.at[1], basis_taps, psf_taps, coeffs, offsets, cover, weights),
            )
        )
    ]
    for load in loads[:2]:
        load.start()

    beside = above.astype(jnp.int32) + below.astype(jnp.int32)

    def greet(semaphore, other, beyond, row):
        pl.semaphore_signal(semaphore, 1, device_id=place(other, slab))
        pl.when(beyond)(lambda: pl.semaphore_signal(semaphore, 1, device_id=place(other, row)))

    barrier = pltpu.get_barrier_semaphore()
    pl.when(below)(lambda: pl.semaphore_signal(barrier, 1, device_id=place(me, slab + 1)))
    for b in range(visits):
        pl.when(me < b)(lambda b=b: greet(barrier, jnp.int32(b), below, slab + 1))

    for load in loads[2:]:
        load.start()

    for dr in (-1, 0, 1):
        for dc in (-1, 0, 1):
            if (dr, dc) == (0, 0):
                continue
            missing = jnp.logical_or(
                jnp.logical_or(slab + dr < 0, slab + dr >= slabs),
                jnp.logical_or(me + dc < 0, me + dc >= visits),
            )

            def blank(dr=dr, dc=dc):
                if dc == 0:
                    tiles[1 + dr] = jnp.zeros((slab_rows, LANES), BF16)
                else:
                    tile_sides[(1 + dc) // 2, 1 + dr] = jnp.zeros((8, LANES), BF16)

            pl.when(missing)(blank)

    ahead = me * (1 + above.astype(jnp.int32)) + above.astype(jnp.int32)
    pl.when(ahead > 0)(lambda: pl.semaphore_wait(barrier, ahead))
    pl.when(above)(lambda: pl.semaphore_signal(ready.at[me], 1, device_id=place(me, slab - 1)))
    for b in range(visits):
        pl.when(me > b)(lambda b=b: greet(ready.at[me], jnp.int32(b), above, slab - 1))

    def await_bytes(ref, size, sem):
        if size > 0:
            part = ref.at[pl.ds(0, size)]
            pltpu.make_async_copy(part, part, sem).wait()

    await_bytes(counted, groups * (1 + visits), loaded.at[0])

    def tile_copy(dr, dc):
        if dc == 0:
            source, target = tiles.at[1], tiles.at[1 - dr]
        else:
            source, target = tile_packs.at[(1 + dc) // 2], tile_sides.at[(1 - dc) // 2, 1 - dr]
        return pltpu.make_async_remote_copy(
            src_ref=source,
            dst_ref=target,
            send_sem=loaded.at[0],
            recv_sem=got_tiles.at[0],
            device_id=place(me + dc, slab + dr),
        )

    def window_copy(other, dr):
        if dr == 0:
            first, height, target = 0, groups, main
        elif dr < 0:
            first, height, target = 0, halo, below_main
        else:
            first, height, target = groups - halo, halo, 1
        return pltpu.make_async_remote_copy(
            src_ref=image.at[pl.ds(first, height), :, pl.ds(pl.multiple_of(other * LANES, LANES), LANES)],
            dst_ref=windows.at[me, pl.ds(target, height)],
            send_sem=loaded.at[0],
            recv_sem=got_windows.at[me],
            device_id=place(other, slab + dr),
        )

    def side_copy(other, dr):
        return pltpu.make_async_remote_copy(
            src_ref=packs.at[other],
            dst_ref=windows.at[me, (below_main + halo, main + groups, 0)[1 + dr]],
            send_sem=loaded.at[0],
            recv_sem=got_windows.at[me],
            device_id=place(other, slab + dr),
        )

    def nearest(k):
        both = 2 * jnp.minimum(me, visits - 1 - me)
        paired = me + ((k + 1) // 2) * (1 if k % 2 == 0 else -1)
        rest = jnp.where(2 * me < visits - 1, k, visits - 1 - k)
        return jnp.where(k <= both, paired, rest)


    def await_windows(sems, other):
        for near in range(3):
            for own in (False, True):
                size = near * (halo + 1) + (0 if own else groups + 1)
                pl.when(jnp.logical_and(beside == near, (other == me) == own))(
                    lambda size=size: await_bytes(windows.at[other], size, sems.at[other])
                )

    def await_blocks(sem, blocks):
        sides = (me > 0).astype(jnp.int32) + (me < visits - 1).astype(jnp.int32)
        for near in range(3):
            for wide in range(3):
                pl.when(jnp.logical_and(beside == near, sides == wide))(
                    lambda size=blocks(near, wide): await_bytes(counted, size, sem)
                )

    def tile_blocks(near, wide):
        return near * groups + wide * (1 + near)

    def sent_blocks(near, wide):
        return tile_blocks(near, wide) + (visits - 1) * (groups + 1) + visits * near * (halo + 1)

    def send_window(other, dr):
        side_copy(other, dr).start()
        window_copy(other, dr).start()

    def send_windows(other, rows=(0, -1, 1)):
        for dr in rows:
            if dr == 0:
                send_window(other, 0)
            else:
                pl.when(above if dr < 0 else below)(lambda dr=dr: send_window(other, dr))

    def send_tiles(dc, rows=(0, -1, 1)):
        for dr in rows:
            if dr == 0:
                tile_copy(0, dc).start()
            else:
                pl.when(above if dr < 0 else below)(lambda dr=dr: tile_copy(dr, dc).start())

    def send_row(dr):
        tile_copy(dr, 0).start()
        send_window(me, dr)

    def await_ready(other):
        pl.semaphore_wait(ready.at[other], 1 + below.astype(jnp.int32))

    def send_first(rows):
        pl.when(me == 1)(lambda: send_tiles(-1, rows))
        pl.when(me > 0)(lambda: send_windows(jnp.int32(0), rows))

    def send_rest(rows):
        pl.when(me > 1)(lambda: send_tiles(-1, rows))
        for b in range(1, visits - 1):
            pl.when(me > b)(lambda b=b: send_windows(jnp.int32(b), rows))

    lane = lax.broadcasted_iota(jnp.int32, (slab_rows, LANES), 1)
    blocks = [image[:, :, b * LANES:(b + 1) * LANES].astype(F32).reshape(slab_rows, LANES) for b in range(visits)]
    own = tiles[1].astype(F32)
    for b in range(visits):
        right, left = blocks[min(b + 1, visits - 1)], blocks[max(b - 1, 0)]
        packs[b] = pack(jnp.where(lane < LANES // 2, right, left), -LANES // groups // 2)
        if b == 0:
            tile_packs[0] = pack(own, 0)
            tile_packs[1] = pack(own, LANES - LANES // groups)
            send_first((-1, 0))

    windows[me, main:main + groups] = image[:, :, pl.ds(pl.multiple_of(me * LANES, LANES), LANES)]
    windows[me, main + groups] = packs[me]
    for load in loads[2:]:
        load.wait()

    out_rows = slab_rows + 2 * (HALO + SHIFT)
    in_rows = 3 * slab_rows
    first = slab_rows - HALO - SHIFT
    rows_parts = []
    for b in range(BASES):
        rows_parts.append(split(band(basis_taps, b, out_rows, LANES, first, False)[:, :in_rows]))
        high, low = split(band(basis_taps, b, WIDE, WIDE, 0, True))
        cols_high[b], cols_low[b] = high, low
    psf_rows = jnp.concatenate(split(band(psf_taps, 0, slab_rows, LANES, HALO, False)[:, :slab_rows + 2 * HALO]), axis=0)
    high, low = split(band(psf_taps, 1, WIDE, WIDE, 0, True)[:, :LANES])
    cols_high[BASES, :, :LANES], cols_high[BASES, :, LANES:] = high, low

    column = lax.broadcasted_iota(jnp.int32, (8, WIDE), 1)
    column = jnp.where(column < WIDE - LANES // 2, column, column - WIDE) + me * LANES
    inside_cols = jnp.logical_and(column >= 0, column < patch_cols)[:1]
    column = column.astype(F32)[:1]
    row = lax.broadcasted_iota(jnp.int32, (out_rows, LANES), 0) + (slab * slab_rows - HALO - SHIFT)
    inside_rows = jnp.logical_and(row >= 0, row < patch_rows)
    row = row.astype(F32)

    def send_below():
        pl.semaphore_wait(ready.at[me], 1)
        send_first((1,))
        send_row(1)
        send_rest((1,))

    pl.when(above)(lambda: send_row(-1))
    send_rest((-1, 0))
    pl.when(below)(send_below)

    def send_next():
        await_ready(me + 1)
        send_tiles(1)
        send_windows(me + 1)

    pl.when(me < visits - 1)(send_next)

    def send_far(other):
        await_ready(other)
        send_windows(other)

    pl.when(me + 2 < visits)(lambda: send_far(me + 2))

    for b in range(3, visits):
        pl.when(me + 2 < b)(lambda b=b: send_far(jnp.int32(b)))

    await_blocks(got_tiles.at[0], tile_blocks)
    lane = lax.broadcasted_iota(jnp.int32, (in_rows, LANES), 1)
    every, width = range(groups), LANES // groups
    centre = tiles[...].astype(F32).reshape(in_rows, LANES)
    right, left = [], []
    for part in range(3):
        left += unpack(tile_sides[0, part], LANES - width, every, groups)
        right += unpack(tile_sides[1, part], 0, every, groups)
    right, left = jnp.concatenate(right, axis=0), jnp.concatenate(left, axis=0)
    field = jnp.concatenate([centre, jnp.where(lane < LANES // 2, right, left)], axis=1).astype(BF16)
    planes = []
    inside = jnp.logical_and(jnp.concatenate([inside_rows, inside_rows], axis=1), inside_cols)
    for b in range(BASES):
        high, low = rows_parts[b]
        passed = mm(high, field) + mm(low, field)
        high, low = split(passed)
        plane = mm(high, cols_high[b]) + (mm(high, cols_low[b]) + mm(low, cols_high[b]))
        planes.append(jnp.where(inside, plane, 0.0).astype(BF16).astype(F32))

    window_rows = slab_rows + 2 * HALO
    total = jnp.zeros((window_rows, WIDE), F32)
    models = []
    for k in range(visits):
        source = nearest(k)
        dy, dx = offsets[0, source], offsets[1, source]
        u = (column - dx.astype(F32) + 0.5) * (2.0 / patch_cols) - 1.0
        w = (row - dy.astype(F32) + 0.5) * (2.0 / patch_rows) - 1.0
        model = None
        for b in range(BASES):
            c = [coeffs[b, source, q] for q in range(6)]
            still = c[0] + w * (c[2] + c[5] * w)
            slope = c[1] + c[4] * w
            both = lambda x: jnp.concatenate([x, x], axis=1)
            term = (both(still) + u * (both(slope) + c[3] * u)) * planes[b]
            model = term if model is None else model + term
        moved = pltpu.roll(model, out_rows - SHIFT - dy, 0)[:window_rows]
        models.append(pltpu.roll(moved, jnp.where(dx > 0, WIDE - dx, -dx), 1))

    y = lax.broadcasted_iota(jnp.int32, (window_rows, WIDE), 0) + (slab * slab_rows - HALO)
    on_patch = jnp.logical_and(jnp.logical_and(y >= 0, y < patch_rows), inside_cols)
    order = [nearest(k) for k in range(visits)]
    shares = [weights[source] * cover[source, slab].astype(F32) for source in order]
    denominator = shares[0]
    for share in shares[1:]:
        denominator = denominator + share
    denominator = jnp.full((slab_rows, LANES), denominator, F32)

    def rows_of(x):
        both = mm(psf_rows, x)
        return both[:slab_rows] + both[slab_rows:]

    passed = None
    for k, source in enumerate(order):
        if k == visits - 1 and k > 0:
            high, low = split(jnp.where(on_patch, total, 0.0))
            passed = rows_of(high) + mm(psf_rows[:slab_rows], low)
        await_windows(got_windows, source)
        window = windows[source].astype(F32)
        columns = []
        for part, chosen in (
            (0, every[-halo:]), (main + groups, every), (below_main + halo, every[:halo])
        ):
            columns += unpack(windows[source, part], -(width // 2), chosen, groups)
        blocks = [window[1:main + groups], window[below_main:below_main + halo]]
        seen = jnp.concatenate(
            [
                jnp.concatenate(blocks, axis=0).reshape(window_rows, LANES),
                jnp.concatenate(columns, axis=0),
            ],
            axis=1,
        )
        difference = seen - models[k]
        if k < visits - 1:
            total = total + shares[k] * difference.astype(BF16).astype(F32)
        else:
            last = shares[k] * rows_of(jnp.where(on_patch, difference, 0.0).astype(BF16))
            passed = last if passed is None else passed + last

    both = mm(jnp.concatenate(split(passed), axis=0), cols_high[BASES])
    filtered = (both[:slab_rows, :LANES] + both[:slab_rows, LANES:]) + both[slab_rows:, :LANES]
    out[...] = filtered / denominator
    await_blocks(loaded.at[0], sent_blocks)


def solution(mesh):
    visits, bands = mesh.shape["visit"], mesh.shape["band"]
    slabs = mesh.shape["tile"] * bands

    def shards(template, images, basis_taps, psf_taps, coeffs, offsets, cover, weights):
        slab_rows = template.shape[0]
        images = images.reshape(images.shape[0], slab_rows // 8, 8, images.shape[2])
        groups, halo = slab_rows // 8, HALO // 8
        sent = 2 * groups + 6 + (visits - 1) * (groups + 1) + 2 * visits * (halo + 1)
        sent = max(sent, groups * (1 + images.shape[3] // LANES))
        vmem = pl.BlockSpec(memory_space=pltpu.VMEM)
        small = (
            basis_taps, psf_taps, coeffs.transpose(1, 0, 2), offsets.transpose(1, 0), cover, weights
        )
        return pl.pallas_call(
            functools.partial(kernel, (visits, slabs, bands)),
            out_shape=pltpu.VMEM(template.shape, F32),
            in_specs=[pl.BlockSpec(memory_space=pl.ANY)] * 8,
            out_specs=vmem,
            scratch_shapes=[
                pltpu.VMEM(images.shape[1:], BF16),
                *[pltpu.SMEM(x.shape, x.dtype) for x in small],
                pltpu.VMEM((3, slab_rows, LANES), BF16),
                pltpu.VMEM((visits, (slab_rows + 2 * HALO) // 8 + 3, 8, LANES), BF16),
                pltpu.VMEM((visits, 8, LANES), BF16),
                pltpu.VMEM((2, 8, LANES), BF16),
                pltpu.VMEM((2, 3, 8, LANES), BF16),
                pltpu.VMEM((BASES + 1, WIDE, WIDE), BF16),
                pltpu.VMEM((BASES, WIDE, WIDE), BF16),
                pltpu.SemaphoreType.DMA((2,)),
                pltpu.VMEM((sent, 8, LANES), BF16),
                pltpu.SemaphoreType.DMA((1,)),
                pltpu.SemaphoreType.DMA((visits,)),
                pltpu.SemaphoreType.REGULAR((visits,)),
            ],
            compiler_params=pltpu.CompilerParams(collective_id=0, has_side_effects=True),
            name="coadd",
        )(template, images, *small)

    placed = (
        P(("grp", "tile", "band"), "visit"),
        P(("grp", "visit"), ("tile", "band"), None),
        P(),
        P(),
        P("grp", None, None),
        P("grp", None),
        P("grp", None),
        P("grp"),
    )
    return jax.shard_map(
        shards,
        mesh=mesh,
        in_specs=placed,
        out_specs=P(("grp", "tile", "band"), "visit"),
        check_vma=False,
    )
```
